32 devices in a mesh: groups: 2 (over x), tm: 16 (over z, y, core).
Axes of the slice: x: 2, y: 2, z: 4, core: 2. Of those that a mesh axis runs over, the one named last changes fastest.
Arguments:
- inputs: bfloat16 [4096, 1280], P(('groups', 'tm')), parts along dimension 0, may hold values from -12 to 12
- ln_gain: float32 [1280], replicated, may hold values from 0.1 to 1.9
- ln_bias: float32 [1280], replicated, may hold values from -3 to 3
- qkv_weight: bfloat16 [1280, 1920], P('tm'), may hold values from -1 to 1
- v_bias: float32 [640], replicated, may hold values from -3 to 3
- out_weight: bfloat16 [640, 1280], P(None, 'tm'), may hold values from -0.25 to 0.25
- out_bias: float32 [1280], replicated, may hold values from -3 to 3
Outputs:
- updated: bfloat16 [4096, 1280], P(('groups', 'tm')), parts along dimension 0
The draws below stay inside these ranges and needn't reach their ends.
There are 2 independent parts, one for each index of `groups`. The reference program is written for one: setup_inputs(seed, part) draws one part's arguments, and reference() takes and returns one part's arrays. A program takes and returns all parts, laid end to end along the dimension named above; an argument that names none is the same for every part. Nothing has to cross between parts.
All inputs are finite; a program needn't handle non-finite values.
Results may differ from the reference program's by a relative error of at most 0.0065.
Values may be sent and summed in bfloat16 or wider, within the bound.
No kernel may reach another device: no remote copies, remote signals or barrier semaphores. Data moves between devices by JAX's collectives and lax.ppermute only.
A program may use at most 192 MiB of HBM per device.

```python
import math
import jax
import jax.numpy as jnp
from jax import lax

D = 1280
HEADS = 10
HEAD_SIZE = 64
TOKENS = 2048


def draw_inputs(key, part):
    key_base = jax.random.fold_in(key, 0)
    drawn = jnp.clip(jax.random.normal(key_base, (TOKENS, D), jnp.float32), -6.0, 6.0)
    return drawn.astype(jnp.bfloat16)


def draw_qkv_weight(key, part):
    head_width = HEADS * HEAD_SIZE
    deviation = jnp.concatenate([jnp.full((2 * head_width,), 1.6, jnp.float32), jnp.ones((head_width,), jnp.float32)]) / math.sqrt(D)
    drawn = jnp.clip(jax.random.normal(key, (D, 3 * head_width), jnp.float32), -4.5, 4.5) * deviation
    return jnp.clip(drawn, -1.0, 1.0).astype(jnp.bfloat16)


def block_scale(stream_key, shape, shards, least, high):
    gain = 1.0
    for axis_at, parts in shards:
        steps = jax.random.uniform(jax.random.fold_in(jax.random.fold_in(stream_key, 6), axis_at), (parts,), jnp.float32, least / len(shards), high / len(shards))
        gain = gain * jnp.repeat(jnp.exp(steps), shape[axis_at] // parts).reshape((-1,) + (1,) * (len(shape) - 1 - axis_at))
    return gain


def bell_draw(stream_key, extent, spread, bound, pieces=(), held_as=jnp.bfloat16):
    loudness = block_scale(stream_key, extent, pieces, -0.22, 0.18) if pieces else 1.0
    array = jax.random.normal(stream_key, extent, jnp.float32) * spread * loudness
    return jnp.minimum(jnp.maximum(array, -bound), bound).astype(held_as)


def setup_inputs(seed: int = 0, part: int = 0) -> dict:
    key_list = jax.random.split(jax.random.key(seed), 8)
    part_keys = jax.random.split(jax.random.fold_in(key_list[7], part), 8)
    return {
        "inputs": draw_inputs(jax.random.fold_in(jax.random.fold_in(key_list[7], part), 71), part),
        "ln_gain": jnp.clip(1.0 + 0.18 * jax.random.normal(key_list[1], (D,), jnp.float32), 0.1, 1.9),
        "ln_bias": bell_draw(key_list[2], (D,), 0.5, 3.0, (), jnp.float32),
        "qkv_weight": draw_qkv_weight(jax.random.fold_in(key_list[7], 71), part),
        "v_bias": bell_draw(key_list[4], (HEADS * HEAD_SIZE,), 0.5, 3.0, (), jnp.float32),
        "out_weight": bell_draw(key_list[5], (HEADS * HEAD_SIZE, D), (HEADS * HEAD_SIZE) ** -0.5, 0.25, ((1, 16),)),
        "out_bias": bell_draw(key_list[6], (D,), 0.5, 3.0, (), jnp.float32),
    }


def layer_norm(inputs, ln_gain, ln_bias):
    widened = inputs.astype(jnp.float32)
    average = lax.optimization_barrier(jnp.mean(widened, -1, keepdims=True))
    centred = widened - average
    variance = lax.optimization_barrier(jnp.mean(centred * centred, -1, keepdims=True))
    return (centred * lax.rsqrt(variance + 1e-05) * ln_gain + ln_bias).astype(jnp.bfloat16)

def reference(inputs, ln_gain, ln_bias, qkv_weight, v_bias, out_weight, out_bias):
    normed = layer_norm(inputs, ln_gain, ln_bias)
    projected = jnp.dot(normed, qkv_weight, preferred_element_type=jnp.float32)
    head_width = HEADS * HEAD_SIZE
    queries = (projected[:, :head_width] * HEAD_SIZE ** (-0.5)).astype(jnp.bfloat16)
    key_rows = projected[:, head_width:2 * head_width].astype(jnp.bfloat16)
    values = (projected[:, 2 * head_width:] + v_bias).astype(jnp.bfloat16)
    block_rows = math.gcd(TOKENS, 512)
    query_blocks = queries.reshape(TOKENS // block_rows, block_rows, HEADS, HEAD_SIZE)
    key_float = key_rows.astype(jnp.float32).reshape(TOKENS, HEADS, HEAD_SIZE)
    value_float = values.astype(jnp.float32).reshape(TOKENS, HEADS, HEAD_SIZE)

    def attend_block(query_block):
        scores = jnp.einsum('qhd,khd->hqk', query_block.astype(jnp.float32), key_float)
        row_max = lax.optimization_barrier(jnp.max(scores, -1, keepdims=True))
        exponent = jnp.exp(scores - row_max)
        row_sum = lax.optimization_barrier(jnp.sum(exponent, -1))
        weights_bf = lax.optimization_barrier(exponent.astype(jnp.bfloat16))
        mixed = jnp.einsum('hqk,khd->hqd', weights_bf.astype(jnp.float32), value_float)
        context = mixed / row_sum[..., None]
        return jnp.transpose(context, (1, 0, 2)).reshape(block_rows, head_width).astype(jnp.bfloat16)
    context = lax.map(attend_block, query_blocks).reshape(TOKENS, head_width)
    projection = jnp.dot(context, out_weight, preferred_element_type=jnp.float32)
    return (inputs.astype(jnp.float32) + projection + out_bias).astype(jnp.bfloat16)
```

```python
import jax
import jax.numpy as jnp
from jax import lax
from jax.sharding import PartitionSpec as P

HEAD_SIZE = 64


def layer_norm(inputs, ln_gain, ln_bias):
    widened = inputs.astype(jnp.float32)
    average = jnp.mean(widened, -1, keepdims=True)
    centred = widened - average
    variance = jnp.mean(centred * centred, -1, keepdims=True)
    return (centred * lax.rsqrt(variance + 1e-05) * ln_gain + ln_bias).astype(jnp.bfloat16)


def attend(state_now, queries, key_part, value_part):
    running_max, running_sum, weighted = state_now
    key_count = key_part.shape[0]
    head_count = queries.shape[1]
    key_heads = key_part.reshape(key_count, head_count, HEAD_SIZE)
    value_heads = value_part.reshape(key_count, head_count, HEAD_SIZE)
    scores = jnp.einsum("qhd,khd->hqk", queries, key_heads, preferred_element_type=jnp.float32)
    new_max = jnp.maximum(running_max, jnp.max(scores, -1))
    rescale = jnp.exp(running_max - new_max)
    exponent = jnp.exp(scores - new_max[..., None])
    running_sum = running_sum * rescale + jnp.sum(exponent, -1)
    weights_bf = exponent.astype(jnp.bfloat16)
    weighted = weighted * rescale[..., None] + jnp.einsum(
        "hqk,khd->hqd", weights_bf, value_heads, preferred_element_type=jnp.float32
    )
    return (new_max, running_sum, weighted)


def empty_state(head_count, row_count):
    return (
        jnp.full((head_count, row_count), -jnp.inf, jnp.float32),
        jnp.zeros((head_count, row_count), jnp.float32),
        jnp.zeros((head_count, row_count, HEAD_SIZE), jnp.float32),
    )


def finish(final_state):
    mixed = final_state[2] / final_state[1][..., None]
    head_count, row_count = (mixed.shape[0], mixed.shape[1])
    return (
        jnp.transpose(mixed, (1, 0, 2))
        .reshape(row_count, head_count * HEAD_SIZE)
        .astype(jnp.bfloat16)
    )


def per_device(inputs, ln_gain, ln_bias, qkv_weight, v_bias, out_weight, out_bias):
    devices = lax.axis_size("tm")
    members = devices // 4
    place = lax.axis_index("tm")
    half = place // (2 * members)

    def swap(value, mask):
        return lax.ppermute(value, "tm", [(i, i ^ mask) for i in range(devices)])

    def swap_half(value):
        return swap(value, 2 * members)

    def swap_member(value, apart):
        return swap(value, 2 * apart)

    def swap_core(value):
        return swap(value, 1)

    head_width = v_bias.shape[0]
    width = head_width // 2
    half_heads = width // HEAD_SIZE
    row_count, features = inputs.shape
    shard = qkv_weight.shape[0]
    out_shard = out_weight.shape[1]

    def columns(value, which):
        picked = [value[:, b * head_width + which * width :][:, :width] for b in range(3)]
        return jnp.concatenate(picked, 1)

    low, high = columns(qkv_weight, 0), columns(qkv_weight, 1)
    mine = jnp.where(half == 0, low, high)
    theirs = jnp.where(half == 0, high, low)
    from_half = swap_half(theirs)
    near = [mine] + [swap_member(mine, d) for d in range(1, members)]
    normed = layer_norm(inputs, ln_gain, ln_bias)
    normed_half = swap_half(normed)
    far = [from_half] + [swap_member(from_half, d) for d in range(1, members)]
    near_core = swap_core(jnp.stack(near))
    far_core = swap_core(jnp.stack(far))

    weight = jnp.zeros((devices * shard, 3 * width), jnp.bfloat16)
    for d in range(members):
        for block, mask in (
            (near[d], 2 * d),
            (far[d], 2 * members ^ 2 * d),
            (near_core[d], 2 * d ^ 1),
            (far_core[d], 2 * members ^ 2 * d ^ 1),
        ):
            weight = lax.dynamic_update_slice_in_dim(weight, block, (place ^ mask) * shard, 0)

    both = jnp.concatenate([normed, normed_half], 0)
    projected = jnp.dot(both, weight, preferred_element_type=jnp.float32)
    bias = lax.dynamic_slice_in_dim(v_bias, half * width, width, 0)
    queries = (projected[:, :width] * HEAD_SIZE ** (-0.5)).astype(jnp.bfloat16)
    key_rows = projected[:, width : 2 * width].astype(jnp.bfloat16)
    values = (projected[:, 2 * width :] + bias).astype(jnp.bfloat16)
    key_values = jnp.concatenate([key_rows, values], 1)

    blocks = [key_values] + [swap_member(key_values, d) for d in range(1, members)]
    query_heads = queries.reshape(2 * row_count, half_heads, HEAD_SIZE)
    state = empty_state(half_heads, 2 * row_count)
    for block in blocks:
        pair = jnp.concatenate([block, swap_core(block)], 0)
        state = attend(state, query_heads, pair[:, :width], pair[:, width:])
    context = finish(state)

    out_mine = out_weight.T
    out_pair = jnp.stack([out_mine, swap_half(out_mine)])
    out_near = [out_pair] + [swap_member(out_pair, d) for d in range(1, members)]
    out_core = swap_core(jnp.stack(out_near))
    out_rows = jnp.zeros((devices * out_shard, head_width), jnp.bfloat16)
    for d in range(members):
        for g in range(2):
            mask = 2 * members * g ^ 2 * d
            out_rows = lax.dynamic_update_slice_in_dim(out_rows, out_near[d][g], (place ^ mask) * out_shard, 0)
            out_rows = lax.dynamic_update_slice_in_dim(out_rows, out_core[d][g], (place ^ mask ^ 1) * out_shard, 0)

    other_context = swap_half(context[row_count:])
    my_part = lax.dynamic_slice_in_dim(out_rows, half * width, width, 1)
    other_part = lax.dynamic_slice_in_dim(out_rows, (1 - half) * width, width, 1)
    dims = (((1,), (1,)), ((), ()))
    projection = lax.dot_general(context[:row_count], my_part, dims, preferred_element_type=jnp.float32)
    projection += lax.dot_general(other_context, other_part, dims, preferred_element_type=jnp.float32)
    return (inputs.astype(jnp.float32) + projection + out_bias).astype(jnp.bfloat16)


def solution(mesh):
    return jax.shard_map(
        per_device,
        mesh=mesh,
        in_specs=(P(("groups", "tm"), None), P(), P(), P("tm", None), P(), P(None, "tm"), P()),
        out_specs=P(("groups", "tm"), None),
        check_vma=False,
    )
```

```python
import functools

import jax
import jax.numpy as jnp
from jax import lax
from jax.experimental import pallas as pl
from jax.experimental.pallas import tpu as pltpu
from jax.sharding import PartitionSpec as P


HEAD_SIZE = 64
LANES = 128
PACKED_ROWS = 16
BLOCKS_PER_CALL = 6


VMEM = pl.BlockSpec(memory_space=pltpu.VMEM)
SMEM = pl.BlockSpec(memory_space=pltpu.SMEM)
ABT = (((1,), (1,)), ((), ()))


def layer_norm(inputs, ln_gain, ln_bias):
    widened = inputs.astype(jnp.float32)
    average = jnp.mean(widened, -1, keepdims=True)
    centred = widened - average
    variance = jnp.mean(centred * centred, -1, keepdims=True)
    return (centred * lax.rsqrt(variance + 1e-05) * ln_gain + ln_bias).astype(jnp.bfloat16)


def stacked_rows(blocks, places):
    rows, width = blocks[0].shape
    whole = jnp.zeros((rows * len(blocks), width), blocks[0].dtype)
    for block, place in zip(blocks, places):
        whole = lax.dynamic_update_slice_in_dim(whole, block, place * rows, 0)
    return whole


def place_rows(places, blocks, whole):
    rows, width = blocks[0].shape
    for i, block in enumerate(blocks):
        start = 0 if len(blocks) == 1 else pl.multiple_of(places[i] * rows, rows)
        whole[pl.ds(start, rows), :width] = block[...]


def as_blocks(blocks, places):
    if blocks[0].shape[0] % PACKED_ROWS:
        blocks, places = [stacked_rows(blocks, places)], places[:1] * 0
    return list(blocks), places


def project(tokens, blocks, places, bias, kv_width):
    rows = sum(t.shape[0] for t in tokens)
    features = tokens[0].shape[1]
    width = blocks[0].shape[1]
    wide = -(-width // LANES) * LANES
    n = len(tokens)

    def kernel(places_ref, bias_ref, *refs):
        token_refs, block_refs = refs[:n], refs[n : n + len(blocks)]
        kv_ref, q_ref, weight = refs[n + len(blocks) :]
        if wide != width:
            weight[:, wide - LANES :] = jnp.zeros((features, LANES), jnp.bfloat16)
        place_rows(places_ref, block_refs, weight)
        at = 0
        for token_ref in token_refs:
            out = pl.ds(at, token_ref.shape[0])
            at += token_ref.shape[0]
            product = jnp.dot(token_ref[...], weight[...], preferred_element_type=jnp.float32)
            kv_ref[out, :] = (product[:, :kv_width] + bias_ref[...]).astype(jnp.bfloat16)
            q_ref[out, :] = (product[:, kv_width:] * HEAD_SIZE ** (-0.5)).astype(jnp.bfloat16)

    return pl.pallas_call(
        kernel,
        out_shape=(
            jax.ShapeDtypeStruct((rows, kv_width), jnp.bfloat16),
            jax.ShapeDtypeStruct((rows, wide - kv_width), jnp.bfloat16),
        ),
        in_specs=[SMEM] + [VMEM] * (1 + n + len(blocks)),
        out_specs=(VMEM, VMEM),
        scratch_shapes=[pltpu.VMEM((features, wide), jnp.bfloat16)],
        name="project",
    )(places, bias, *tokens, *blocks)


def lane_half(shape):
    return lax.broadcasted_iota(jnp.int32, shape, 1) // HEAD_SIZE


def head_lanes(heads):
    values_from = heads + heads % 2
    out = []
    for head in range(heads):
        v_at = heads if heads % 2 and head == heads - 1 else values_from + head
        out.append((head // 2, head % 2, v_at // 2, v_at % 2))
    return out


def attend(queries, blocks, heads, state, last):
    rows = queries.shape[0]
    width = heads * HEAD_SIZE
    stats = jax.ShapeDtypeStruct((rows, LANES), jnp.float32)
    sums = jax.ShapeDtypeStruct((rows, heads * LANES), jnp.float32)
    given = [] if state is None else list(state)

    def kernel(q_ref, *refs):
        old = refs[: len(given)]
        block_refs = refs[len(given) : len(given) + len(blocks)]
        outs = refs[len(given) + len(blocks) :]
        mixed_tiles = []
        for head, (k_tile, k_half, v_tile, v_half) in enumerate(head_lanes(heads)):
            query = q_ref[:, k_tile * LANES :][:, :LANES]
            query = jnp.where(lane_half(query.shape) == k_half, query, jnp.zeros_like(query))
            scores = []
            for block in block_refs:
                keys = block[:, k_tile * LANES :][:, :LANES]
                scores.append(lax.dot_general(query, keys, ABT, preferred_element_type=jnp.float32))
            tops = [jnp.max(s, -1, keepdims=True) for s in scores]
            if old:
                tops.append(old[0][:, head : head + 1])
            top = functools.reduce(jnp.maximum, tops)
            total, mixed = None, None
            for block, score in zip(block_refs, scores):
                exponent = jnp.exp(score - top)
                values = block[:, v_tile * LANES :][:, :LANES]
                part = jnp.dot(exponent.astype(jnp.bfloat16), values, preferred_element_type=jnp.float32)
                some = jnp.sum(exponent, -1, keepdims=True)
                total = some if total is None else total + some
                mixed = part if mixed is None else mixed + part
            if old:
                rescale = jnp.exp(old[0][:, head : head + 1] - top)
                total += old[1][:, head : head + 1] * rescale
                mixed += old[2][:, head * LANES :][:, :LANES] * rescale
            if last:
                mixed = mixed / total
                if v_half != head % 2:
                    mixed = pltpu.roll(mixed, HEAD_SIZE, 1)
                mixed_tiles.append(mixed)
                continue
            outs[0][:, head : head + 1] = top
            outs[1][:, head : head + 1] = total
            outs[2][:, head * LANES : (head + 1) * LANES] = mixed
        if last:
            for at in range(0, heads, 2):
                tile = mixed_tiles[at]
                if at + 1 < heads:
                    tile = jnp.where(lane_half(tile.shape) == 0, tile, mixed_tiles[at + 1])
                    outs[0][:, at * HEAD_SIZE : at * HEAD_SIZE + LANES] = tile.astype(jnp.bfloat16)
                else:
                    outs[0][:, at * HEAD_SIZE :] = tile[:, :HEAD_SIZE].astype(jnp.bfloat16)

    out = jax.ShapeDtypeStruct((rows, width), jnp.bfloat16) if last else (stats, stats, sums)
    return pl.pallas_call(
        kernel,
        out_shape=out,
        in_specs=[VMEM] * (1 + len(given) + len(blocks)),
        out_specs=VMEM if last else (VMEM,) * 3,
        name="attend",
    )(queries, *given, *blocks)


def gather_rows(blocks, places):
    blocks, places = as_blocks(blocks, places)
    rows = sum(b.shape[0] for b in blocks)

    def kernel(places_ref, *refs):
        place_rows(places_ref, refs[:-1], refs[-1])

    return pl.pallas_call(
        kernel,
        out_shape=jax.ShapeDtypeStruct((rows, blocks[0].shape[1]), blocks[0].dtype),
        in_specs=[SMEM] + [VMEM] * len(blocks),
        out_specs=VMEM,
        name="gather_rows",
    )(places, *blocks)


def finish(half, mine, other, weight_rows, inputs, out_bias):
    def kernel(half_ref, mine_ref, other_ref, weight_ref, inputs_ref, bias_ref, out_ref):
        first = half_ref[0] == 0
        a, b = mine_ref[...], other_ref[...]
        context = jnp.where(first, jnp.concatenate([a, b], 1), jnp.concatenate([b, a], 1))
        product = lax.dot_general(context, weight_ref[...], ABT, preferred_element_type=jnp.float32)
        out_ref[...] = (inputs_ref[...].astype(jnp.float32) + product + bias_ref[...]).astype(jnp.bfloat16)

    return pl.pallas_call(
        kernel,
        out_shape=jax.ShapeDtypeStruct(inputs.shape, inputs.dtype),
        in_specs=[SMEM] + [VMEM] * 5,
        out_specs=VMEM,
        name="finish",
    )(half.reshape(1), mine, other, weight_rows, inputs, out_bias.reshape(1, -1))


def head_order(queries, keys, values, axis):
    width = values.shape[axis]
    if (width // HEAD_SIZE) % 2:
        split = lax.split(values, (width - HEAD_SIZE, HEAD_SIZE), axis)
        values = jnp.concatenate(split[::-1], axis)
    return jnp.concatenate([keys, values] + ([] if queries is None else [queries]), axis)


def per_device(inputs, ln_gain, ln_bias, qkv_weight, v_bias, out_weight, out_bias):
    devices = lax.axis_size("tm")
    members = devices // 4
    place = lax.axis_index("tm")
    half = place // (2 * members)

    def swap(value, mask):
        return lax.ppermute(value, "tm", [(i, i ^ mask) for i in range(devices)])

    across = 2 * members
    head_width = v_bias.shape[0]
    width = head_width // 2
    heads = width // HEAD_SIZE
    row_count = inputs.shape[0]
    others = range(1, members)

    def columns(value, which):
        parts = [value[:, b * head_width + which * width :][:, :width] for b in range(3)]
        return head_order(*parts, 1)

    low, high = columns(qkv_weight, 0), columns(qkv_weight, 1)
    mine = jnp.where(half == 0, low, high)
    theirs = jnp.where(half == 0, high, low)
    from_half = swap(theirs, across)
    near = [mine] + [swap(mine, 2 * d) for d in others]
    normed = layer_norm(inputs, ln_gain, ln_bias)
    normed_half = swap(normed, across)
    far = [from_half] + [swap(from_half, 2 * d) for d in others]
    near_core = [swap(near[d], 1) for d in range(members)]
    far_core = [swap(far[d], 1) for d in range(members)]
    masks = [2 * d ^ across * g ^ c for c in range(2) for g in range(2) for d in range(members)]
    places = place ^ jnp.array(masks, jnp.int32)
    blocks, block_places = as_blocks(near + far + near_core + far_core, places)

    my_bias = lax.dynamic_slice_in_dim(v_bias, half * width, width, 0)
    bias = head_order(None, jnp.zeros_like(my_bias), my_bias, 0).reshape(1, -1)
    key_values, queries = project([normed, normed_half], blocks, block_places, bias, 2 * width)

    pieces = [key_values] + [swap(key_values, 2 * d) for d in others]
    pairs = []
    for piece in pieces:
        pairs += [piece, swap(piece, 1)]
    state = None
    for at in range(0, len(pairs), BLOCKS_PER_CALL):
        chunk = pairs[at : at + BLOCKS_PER_CALL]
        state = attend(queries, chunk, heads, state, at + len(chunk) == len(pairs))
    context = state

    out_mine = out_weight.T
    out_half = [out_mine, swap(out_mine, across)]
    stage = jnp.concatenate(out_half, 0)
    shard = out_mine.shape[0]
    got = [stage] + [swap(stage, 2 * d) for d in others]
    whole_pieces = got + [swap(got[d], 1) for d in range(members)]
    out_blocks = [p[g * shard : (g + 1) * shard] for p in whole_pieces for g in range(2)]
    out_masks = [2 * d ^ across * g ^ c for c in range(2) for d in range(members) for g in range(2)]
    out_rows = gather_rows(out_blocks, place ^ jnp.array(out_masks, jnp.int32))

    other_context = swap(context[row_count:], across)
    return finish(half, context[:row_count], other_context, out_rows, inputs, out_bias)


def solution(mesh):
    return jax.shard_map(
        per_device,
        mesh=mesh,
        in_specs=(P(("groups", "tm"), None), P(), P(), P("tm", None), P(), P(None, "tm"), P()),
        out_specs=P(("groups", "tm"), None),
        check_vma=False,
    )
```
